32 devices in a mesh: fsdp: 8 (over z, y), seq: 4 (over x, core).
Axes of the slice: x: 2, y: 2, z: 4, core: 2. Of those that a mesh axis runs over, the one named last changes fastest.
Arguments:
- layer_input: bfloat16 [8, 512, 768], P('fsdp', 'seq'), may hold values from -8 to 8
- valid_lengths: int32 [8], P('fsdp'), may hold values from 64 to 512, as said below
- w_qkv: bfloat16 [1769472], P(('fsdp', 'seq')), may hold values from -1 to 1
- w_out: bfloat16 [589824], P(('fsdp', 'seq')), may hold values from -2.5 to 2.5
- w_up: bfloat16 [2359296], P(('fsdp', 'seq')), may hold values from -0.21875 to 0.21875
- w_down: bfloat16 [2359296], P(('fsdp', 'seq')), may hold values from -0.109375 to 0.109375
- vectors: bfloat16 [9216], P(('fsdp', 'seq')), may hold values from -2 to 2
- cotangent: bfloat16 [8, 512, 768], P('fsdp', 'seq'), may hold values from -6 to 6
Outputs:
- layer_output: bfloat16 [8, 512, 768], P('fsdp', 'seq')
- input_grad: float32 [8, 512, 768], P('fsdp', 'seq')
- grad_qkv: float32 [1769472], P(('fsdp', 'seq'))
- grad_out: float32 [589824], P(('fsdp', 'seq'))
- grad_up: float32 [2359296], P(('fsdp', 'seq'))
- grad_down: float32 [2359296], P(('fsdp', 'seq'))
- grad_vectors: float32 [9216], P(('fsdp', 'seq'))
The draws below stay inside these ranges and needn't reach their ends.
Inputs may be any that keep to these rules, and one draw needn't show every extreme that they name: `valid_lengths`: positions from a sequence's valid length on are padding; some sequence has length exactly 512, some exactly 64.
All inputs are finite; a program needn't handle non-finite values.
Results may differ from the reference program's by a relative error of at most 0.012.
The reference program's roundings to bfloat16 on the way count: a program that leaves them out, or rounds other values in their place, can miss the bound.
Values may be sent and summed in bfloat16 or wider, within the bound.
No kernel may reach another device: no remote copies, remote signals or barrier semaphores. Data moves between devices by JAX's collectives and lax.ppermute only.
A program may use at most 192 MiB of HBM per device.

```python
import math
import jax
import jax.numpy as jnp
from jax import lax

D = 768
H = 12
FF = 3072
HD = 64
LEN = 512
SEQS = 8


def draw_layer_input(key, part):
    base = jax.random.normal(key, (SEQS, LEN, D), jnp.float32)
    return jnp.clip(base, -8.0, 8.0).astype(jnp.bfloat16)


def draw_valid_lengths(key, part):
    lengths = jax.random.randint(jax.random.fold_in(key, 21), (SEQS,), LEN // 8, LEN + 1)
    order = jax.random.permutation(jax.random.fold_in(key, 22), SEQS)
    places = jnp.arange(SEQS)
    lengths = jnp.where(places == order[0], LEN, lengths)
    lengths = jnp.where(places == order[1], LEN // 8, lengths)
    return lengths.astype(jnp.int32)


def draw_w_qkv(key, part):
    matrix = jax.random.normal(jax.random.fold_in(key, 31), (D, 3 * D), jnp.float32) / D ** 0.5
    return jnp.clip(matrix, -1.0, 1.0).reshape(-1).astype(jnp.bfloat16)


def draw_vectors(key, part):
    total = 8 * D + FF
    biases = 0.5 * jax.random.normal(jax.random.fold_in(key, 41), (total,), jnp.float32)
    gains = jax.random.uniform(jax.random.fold_in(key, 42), (total,), jnp.float32, 0.5, 1.5)
    places = jnp.arange(total)
    is_gain = (places >= 3 * D) & (places < 4 * D) | (places >= 6 * D) & (places < 7 * D)
    return jnp.clip(jnp.where(is_gain, gains, biases), -2.0, 2.0).astype(jnp.bfloat16)


def block_levels(rng, dims, cuts, smallest, top_value):
    def one(position, blocks):
        heights = jax.random.uniform(jax.random.fold_in(jax.random.fold_in(rng, 6), position), (blocks,), jnp.float32, smallest / len(cuts), top_value / len(cuts))
        return jnp.repeat(jnp.exp(heights), dims[position] // blocks).reshape((-1,) + (1,) * (len(dims) - position - 1))

    level = one(*cuts[0])
    for cut in cuts[1:]:
        level = level * one(*cut)
    return level


def gaussian(key, dims, scale, limit, cuts=(), kind=jnp.bfloat16):
    entries = jax.random.normal(key, dims, jnp.float32) * scale
    if len(cuts) > 0:
        entries = block_levels(key, dims, cuts, -0.22, 0.18) * entries
    return jnp.clip(entries, min=-limit, max=limit).astype(kind)


def setup_inputs(seed: int = 0) -> dict:
    streams_of = jax.random.split(jax.random.key(seed), 9)
    layer_input = draw_layer_input(jax.random.fold_in(streams_of[8], 71), 0)
    valid_lengths = draw_valid_lengths(jax.random.fold_in(streams_of[8], 71), 0)
    w_qkv = draw_w_qkv(jax.random.fold_in(streams_of[8], 71), 0)
    w_out = gaussian(streams_of[3], (D * D,), (max(4 * D // LEN, 1)) ** -0.5, 2.5, ((0, 32),))
    w_up = gaussian(streams_of[4], (D * FF,), D ** -0.5, 0.21875, ((0, 32),))
    w_down = gaussian(streams_of[5], (FF * D,), FF ** -0.5, 0.109375, ((0, 32),))
    vectors = draw_vectors(jax.random.fold_in(streams_of[8], 71), 0)
    cotangent = gaussian(streams_of[7], (SEQS, LEN, D), 1.0, 6.0, ((0, 8), (1, 4)))
    return dict(layer_input=layer_input, valid_lengths=valid_lengths, w_qkv=w_qkv, w_out=w_out, w_up=w_up, w_down=w_down, vectors=vectors, cotangent=cotangent)


NEG = -1e+30
EPS = 1e-06
ROOT_HALF = 0.7071067811865476
INV_ROOT_TAU = 0.3989422804014327

def layer_norm(value, gain, shift):
    center = value - lax.optimization_barrier(jnp.mean(value, axis=-1, keepdims=True))
    rstd = lax.rsqrt(lax.optimization_barrier(jnp.mean(center * center, axis=-1, keepdims=True)) + EPS)
    normed = center * rstd
    return (normed * gain + shift, normed, rstd)

def norm_back(grad, normed, rstd, gain):
    scaled = grad * gain
    return rstd * (scaled - lax.optimization_barrier(jnp.mean(scaled, axis=-1, keepdims=True)) - normed * lax.optimization_barrier(jnp.mean(scaled * normed, axis=-1, keepdims=True)))

def gelu_exact(value):
    return 0.5 * value * (1.0 + lax.erf(value * ROOT_HALF))

def gelu_slope(value):
    return 0.5 * (1.0 + lax.erf(value * ROOT_HALF)) + value * jnp.exp(-0.5 * value * value) * INV_ROOT_TAU

def one_sequence(params, rows, length, dout):
    wqkv, wo, w1, w2, parts = params
    q_bias, v_bias, o_bias, gain_one, shift_one, down_bias, gain_two, shift_two, up_bias = parts
    scale = 1.0 / math.sqrt(HD)
    qkv = jnp.dot(rows, wqkv, preferred_element_type=jnp.float32) + jnp.concatenate([q_bias, jnp.zeros_like(q_bias), v_bias])
    query = qkv[:, :D].astype(jnp.bfloat16)
    keys = qkv[:, D:2 * D].astype(jnp.bfloat16)
    values = qkv[:, 2 * D:].astype(jnp.bfloat16)
    qh = query.reshape(LEN, H, HD).astype(jnp.float32)
    kh = keys.reshape(LEN, H, HD).astype(jnp.float32)
    vh = values.reshape(LEN, H, HD).astype(jnp.float32)
    keep = jnp.arange(LEN) < length
    scores = jnp.einsum('qhd,khd->hqk', qh, kh) * scale
    scores = jnp.where(keep[None, None, :], scores, NEG)
    top = lax.optimization_barrier(jnp.max(scores, axis=-1, keepdims=True))
    expo = jnp.exp(scores - top)
    total = lax.optimization_barrier(jnp.sum(expo, axis=-1, keepdims=True))
    lse = top + jnp.log(total)
    probs = (expo / total).astype(jnp.bfloat16)
    context = jnp.einsum('hqk,khd->qhd', probs.astype(jnp.float32), vh).reshape(LEN, D).astype(jnp.bfloat16)
    first = rows.astype(jnp.float32) + jnp.dot(context, wo, preferred_element_type=jnp.float32) + o_bias
    mid, normed_one, rstd_one = layer_norm(first, gain_one, shift_one)
    mid_b = mid.astype(jnp.bfloat16)
    upper = jnp.dot(mid_b, w1, preferred_element_type=jnp.float32) + up_bias
    active = gelu_exact(upper).astype(jnp.bfloat16)
    second = mid + jnp.dot(active, w2, preferred_element_type=jnp.float32) + down_bias
    result, normed_two, rstd_two = layer_norm(second, gain_two, shift_two)
    output = result.astype(jnp.bfloat16)
    grad = dout.astype(jnp.float32)
    d_gain_two = lax.optimization_barrier(jnp.sum(grad * normed_two, axis=0))
    d_shift_two = lax.optimization_barrier(jnp.sum(grad, axis=0))
    d_second = norm_back(grad, normed_two, rstd_two, gain_two)
    d_down_bias = lax.optimization_barrier(jnp.sum(d_second, axis=0))
    d_second_b = d_second.astype(jnp.bfloat16)
    d_w2 = jnp.dot(active.T, d_second_b, preferred_element_type=jnp.float32)
    d_upper = jnp.dot(d_second_b, w2.T, preferred_element_type=jnp.float32) * gelu_slope(upper)
    d_up_bias = lax.optimization_barrier(jnp.sum(d_upper, axis=0))
    d_upper_b = d_upper.astype(jnp.bfloat16)
    d_w1 = jnp.dot(mid_b.T, d_upper_b, preferred_element_type=jnp.float32)
    d_mid = d_second + jnp.dot(d_upper_b, w1.T, preferred_element_type=jnp.float32)
    d_gain_one = lax.optimization_barrier(jnp.sum(d_mid * normed_one, axis=0))
    d_shift_one = lax.optimization_barrier(jnp.sum(d_mid, axis=0))
    d_first = norm_back(d_mid, normed_one, rstd_one, gain_one)
    d_o_bias = lax.optimization_barrier(jnp.sum(d_first, axis=0))
    d_first_b = d_first.astype(jnp.bfloat16)
    d_wo = jnp.dot(context.T, d_first_b, preferred_element_type=jnp.float32)
    d_context = jnp.dot(d_first_b, wo.T, preferred_element_type=jnp.float32).astype(jnp.bfloat16)
    dch = d_context.reshape(LEN, H, HD).astype(jnp.float32)
    cth = context.reshape(LEN, H, HD).astype(jnp.float32)
    again = jnp.einsum('qhd,khd->hqk', qh, kh) * scale
    again = jnp.where(keep[None, None, :], again, NEG)
    prob = jnp.exp(again - lse)
    prob_b = prob.astype(jnp.bfloat16).astype(jnp.float32)
    d_vh = jnp.einsum('hqk,qhd->khd', prob_b, dch)
    d_prob = jnp.einsum('qhd,khd->hqk', dch, vh)
    delta = jnp.transpose(lax.optimization_barrier(jnp.sum(dch * cth, axis=-1)), (1, 0))[:, :, None]
    d_scores = (prob * (d_prob - delta) * scale).astype(jnp.bfloat16).astype(jnp.float32)
    d_qh = jnp.einsum('hqk,khd->qhd', d_scores, kh).reshape(LEN, D)
    d_kh = jnp.einsum('hqk,qhd->khd', d_scores, qh).reshape(LEN, D)
    d_vh = d_vh.reshape(LEN, D)
    d_q_bias = lax.optimization_barrier(jnp.sum(d_qh, axis=0))
    d_v_bias = lax.optimization_barrier(jnp.sum(d_vh, axis=0))
    d_qkv = jnp.concatenate([d_qh, d_kh, d_vh], axis=1).astype(jnp.bfloat16)
    d_wqkv = jnp.dot(rows.T, d_qkv, preferred_element_type=jnp.float32)
    d_rows = d_first + jnp.dot(d_qkv, wqkv.T, preferred_element_type=jnp.float32)
    d_vec = jnp.concatenate([d_q_bias, d_v_bias, d_o_bias, d_gain_one, d_shift_one, d_down_bias, d_gain_two, d_shift_two, d_up_bias])
    return (output, d_rows, (d_wqkv, d_wo, d_w1, d_w2, d_vec))

def reference(layer_input, valid_lengths, w_qkv, w_out, w_up, w_down, vectors, cotangent):
    flat = vectors.astype(jnp.float32)
    parts = tuple((flat[i * D:(i + 1) * D] for i in range(8))) + (flat[8 * D:],)
    params = (w_qkv.reshape(D, 3 * D), w_out.reshape(D, D), w_up.reshape(D, FF), w_down.reshape(FF, D), parts)
    init = (jnp.zeros((D, 3 * D), jnp.float32), jnp.zeros((D, D), jnp.float32), jnp.zeros((D, FF), jnp.float32), jnp.zeros((FF, D), jnp.float32), jnp.zeros((8 * D + FF,), jnp.float32))

    def step(carry, item):
        rows, length, dout = item
        output, d_rows, grads = one_sequence(params, rows, length, dout)
        return (tuple((a + b for a, b in zip(carry, grads))), (output, d_rows))
    sums, (outputs, d_inputs) = lax.scan(step, init, (layer_input, valid_lengths, cotangent))
    return (outputs, d_inputs, sums[0].reshape(-1), sums[1].reshape(-1), sums[2].reshape(-1), sums[3].reshape(-1), sums[4])
```

```python
import math

import jax
import jax.numpy as jnp
from jax import lax
from jax.sharding import Mesh
from jax.sharding import PartitionSpec as P

H = 12
NEG = -1e30
EPS = 1e-06
ROOT_HALF = 0.7071067811865476
INV_ROOT_TAU = 0.3989422804014327

BF = jnp.bfloat16
F32 = jnp.float32
SEQ = ("x", "core")
FSDP = ("z", "y")
ALL = ("z", "y", "x", "core")


def dot(a, b, ca, cb):
    return lax.dot_general(a, b, (((ca,), (cb,)), ((), ())), preferred_element_type=F32)


def shift(value, axis, step):
    n = lax.axis_size(axis)
    return lax.ppermute(value, axis, [(i, (i + step) % n) for i in range(n)])


def pick(value, index):
    return lax.dynamic_index_in_dim(value, index, 0, keepdims=False)


def gather_pieces(value, axis):
    return [value] + [shift(value, axis, k) for k in range(1, lax.axis_size(axis))]


def place(pieces, axis):
    n = len(pieces)
    me = lax.axis_index(axis)
    if n == 2:
        a, b = pieces
        return jnp.stack([jnp.where(me == 0, a, b), jnp.where(me == 0, b, a)])
    out = jnp.zeros((n,) + pieces[0].shape, pieces[0].dtype)
    for k, piece in enumerate(pieces):
        out = lax.dynamic_update_index_in_dim(out, piece, (me - k) % n, 0)
    return out


def scatter_pieces(blocks, axis):
    n = lax.axis_size(axis)
    me = lax.axis_index(axis)
    own = pick(blocks, me)
    return own, [shift(pick(blocks, (me + k) % n), axis, k) for k in range(1, n)]


def gather_seq(value):
    rows, width = value.shape
    ax = gather_pieces(value, "x")
    both = [place([p, shift(p, "core", 1)], "core") for p in ax]
    out = place(both, "x")
    return out.reshape(-1, width)


def reduce_seq(part):
    width = part.shape[-1]
    nx, nc = lax.axis_size("x"), lax.axis_size("core")
    blocks = part.reshape(nx, nc, -1, width)
    core = lax.axis_index("core")
    by_core = jnp.moveaxis(blocks, 1, 0)
    own = pick(by_core, core)
    for k in range(1, nc):
        own = own + shift(pick(by_core, (core + k) % nc).astype(BF), "core", k).astype(F32)
    me = lax.axis_index("x")
    total = pick(own, me)
    for k in range(1, nx):
        total = total + shift(pick(own, (me + k) % nx).astype(BF), "x", k).astype(F32)
    return total


def gather_fsdp(value):
    rows, width = value.shape
    nz, ny = lax.axis_size("z"), lax.axis_size("y")
    if nz > 8:
        return lax.all_gather(value, FSDP, axis=0, tiled=True)
    z, y = lax.axis_index("z"), lax.axis_index("y")
    out = jnp.zeros((nz * ny, rows, width), value.dtype)
    for k, piece in enumerate(gather_pieces(value, "z")):
        for j, sub in enumerate(gather_pieces(piece, "y")):
            out = lax.dynamic_update_index_in_dim(
                out, sub, ((z - k) % nz) * ny + (y - j) % ny, 0
            )
    return out.reshape(nz * ny * rows, width)


def reduce_fsdp(part):
    width = part.shape[-1]
    nz, ny = lax.axis_size("z"), lax.axis_size("y")
    blocks = jnp.moveaxis(part.reshape(nz, ny, -1, width), 1, 0)
    y, z = lax.axis_index("y"), lax.axis_index("z")
    own = pick(blocks, y)
    for j in range(1, ny):
        own = own + shift(pick(blocks, (y + j) % ny).astype(BF), "y", j).astype(F32)
    if nz > 8:
        got = lax.all_to_all(own.astype(BF), "z", 0, 0, tiled=True)
        return jnp.sum(got.astype(F32), axis=0)
    total = pick(own, z)
    for k in range(1, nz):
        total = total + shift(pick(own, (z + k) % nz).astype(BF), "z", k).astype(F32)
    return total


def exchange_seq(blocks):
    own, got = scatter_pieces(blocks, SEQ)
    return place([own] + got, SEQ)


def layer_norm(value):
    center = value - jnp.mean(value, axis=-1, keepdims=True)
    rstd = lax.rsqrt(jnp.mean(center * center, axis=-1, keepdims=True) + EPS)
    return center * rstd, rstd


def norm_back(grad, normed, rstd, gain):
    scaled = grad * gain
    return rstd * (
        scaled
        - jnp.mean(scaled, axis=-1, keepdims=True)
        - normed * jnp.mean(scaled * normed, axis=-1, keepdims=True)
    )


def on_device(layer_input, valid_lengths, w_qkv, w_out, w_up, w_down, vectors, cotangent):
    batch, rows, width = layer_input.shape
    assert batch == 1
    nseq = lax.axis_size(SEQ)
    nf = lax.axis_size(FSDP)
    nall = nseq * nf
    s = lax.axis_index(SEQ)
    f = lax.axis_index(FSDP)
    flat_index = f * nseq + s
    span = rows * nseq
    hidden = w_up.shape[0] * nall // width
    head = width // H
    mine = H // nseq
    hw = mine * head
    hid = hidden // nseq
    scale = 1.0 / math.sqrt(head)
    into = [(b, (b % nf) * nseq + b // nf) for b in range(nall)]
    back = [(d, b) for b, d in into]

    r = width // nall
    tokens = layer_input.reshape(rows, width)
    x_full = gather_seq(tokens)
    wq_blocks = jnp.transpose(w_qkv.reshape(r, 3, nseq, hw), (2, 0, 1, 3)).reshape(nseq, r, 3 * hw)
    wqkv = gather_fsdp(exchange_seq(wq_blocks).reshape(nseq * r, 3 * hw))
    up_blocks = jnp.transpose(w_up.reshape(r, nseq, hid), (1, 0, 2))
    wu = exchange_seq(up_blocks).reshape(nseq * r, hid)
    wo_mine = lax.ppermute(w_out.reshape(r, width), ALL, into)
    wd_mine = lax.ppermute(w_down.reshape(hidden // nall, width), ALL, into)
    wo = gather_fsdp(wo_mine)
    w1 = gather_fsdp(wu)
    w2 = gather_fsdp(wd_mine)

    vec = vectors
    if lax.axis_size("z") > 8:
        vec = lax.all_gather(vec, ALL, axis=0, tiled=True)
    else:
        for axis in ("core", "x", "y", "z"):
            vec = place(gather_pieces(vec, axis), axis).reshape(-1)
    flat = vec.astype(F32)
    q_bias, v_bias, o_bias, gain_one, shift_one, down_bias, gain_two, shift_two = [
        flat[i * width : (i + 1) * width] for i in range(8)
    ]
    up_bias = lax.dynamic_slice_in_dim(flat, 8 * width + s * hid, hid)
    q_bias = lax.dynamic_slice_in_dim(q_bias, s * hw, hw)
    v_bias = lax.dynamic_slice_in_dim(v_bias, s * hw, hw)

    qkv = dot(x_full, wqkv, 1, 0) + jnp.concatenate([q_bias, jnp.zeros_like(q_bias), v_bias])
    query = qkv[:, :hw].astype(BF)
    keys = qkv[:, hw : 2 * hw].astype(BF)
    values = qkv[:, 2 * hw :].astype(BF)
    keep = jnp.arange(span) < valid_lengths[0]
    qh = query.reshape(span, mine, head)
    kh = keys.reshape(span, mine, head)
    vh = values.reshape(span, mine, head)
    scores = jnp.einsum("qhd,khd->hqk", qh, kh, preferred_element_type=F32) * scale
    scores = jnp.where(keep[None, None, :], scores, NEG)
    top = jnp.max(scores, axis=-1, keepdims=True)
    expo = jnp.exp(scores - top)
    total = jnp.sum(expo, axis=-1, keepdims=True)
    lse = top + jnp.log(total)
    probs = (expo / total).astype(BF)
    context = jnp.einsum("hqk,khd->qhd", probs, vh, preferred_element_type=F32)
    context = context.reshape(span, hw).astype(BF)

    first = tokens.astype(F32) + reduce_seq(dot(context, wo, 1, 0)) + o_bias
    normed_one, rstd_one = layer_norm(first)
    mid = normed_one * gain_one + shift_one
    mid_b = gather_seq(mid.astype(BF))
    upper = dot(mid_b, w1, 1, 0) + up_bias
    cdf = 0.5 * (1.0 + lax.erf(upper * ROOT_HALF))
    active = (upper * cdf).astype(BF)
    second = mid + reduce_seq(dot(active, w2, 1, 0)) + down_bias
    normed_two, rstd_two = layer_norm(second)
    layer_output = (normed_two * gain_two + shift_two).astype(BF).reshape(batch, rows, width)

    grad = cotangent.reshape(rows, width).astype(F32)
    d_gain_two = jnp.sum(grad * normed_two, axis=0)
    d_shift_two = jnp.sum(grad, axis=0)
    d_second = norm_back(grad, normed_two, rstd_two, gain_two)
    d_down_bias = jnp.sum(d_second, axis=0)
    d_second_b = gather_seq(d_second.astype(BF))
    slope = cdf + upper * jnp.exp(-0.5 * upper * upper) * INV_ROOT_TAU
    d_upper = dot(d_second_b, w2, 1, 1) * slope
    d_up_bias = jnp.sum(d_upper, axis=0)
    d_upper_b = d_upper.astype(BF)
    d_mid = d_second + reduce_seq(dot(d_upper_b, w1, 1, 1))
    d_w2 = reduce_fsdp(dot(active, d_second_b, 0, 0))
    d_w1 = reduce_fsdp(dot(mid_b, d_upper_b, 0, 0))
    grad_down = lax.ppermute(d_w2, ALL, back).reshape(-1)
    grad_up = exchange_seq(d_w1.reshape(nseq, r, hid))
    grad_up = jnp.transpose(grad_up, (1, 0, 2)).reshape(-1)

    d_gain_one = jnp.sum(d_mid * normed_one, axis=0)
    d_shift_one = jnp.sum(d_mid, axis=0)
    d_first = norm_back(d_mid, normed_one, rstd_one, gain_one)
    d_o_bias = jnp.sum(d_first, axis=0)
    d_first_b = gather_seq(d_first.astype(BF))
    d_context = dot(d_first_b, wo, 1, 1).astype(BF)
    d_wo = reduce_fsdp(dot(context, d_first_b, 0, 0))
    grad_out = lax.ppermute(d_wo, ALL, back).reshape(-1)

    dch = d_context.reshape(span, mine, head)
    cth = context.reshape(span, mine, head)
    prob = jnp.exp(scores - lse)
    prob_b = prob.astype(BF)
    d_vh = jnp.einsum("hqk,qhd->khd", prob_b, dch, preferred_element_type=F32)
    d_prob = jnp.einsum("qhd,khd->hqk", dch, vh, preferred_element_type=F32)
    delta = jnp.sum(dch.astype(F32) * cth.astype(F32), axis=-1)
    delta = jnp.transpose(delta, (1, 0))[:, :, None]
    d_scores = (prob * (d_prob - delta) * scale).astype(BF)
    d_qh = jnp.einsum("hqk,khd->qhd", d_scores, kh, preferred_element_type=F32)
    d_kh = jnp.einsum("hqk,qhd->khd", d_scores, qh, preferred_element_type=F32)
    d_q = d_qh.reshape(span, hw)
    d_k = d_kh.reshape(span, hw)
    d_v = d_vh.reshape(span, hw)
    d_q_bias = jnp.sum(d_q, axis=0)
    d_v_bias = jnp.sum(d_v, axis=0)
    d_qkv = jnp.concatenate([d_q, d_k, d_v], axis=1).astype(BF)
    input_grad = d_first + reduce_seq(dot(d_qkv, wqkv, 1, 1))
    input_grad = input_grad.reshape(batch, rows, width)
    d_wqkv = reduce_fsdp(dot(x_full, d_qkv, 0, 0))
    grad_qkv = exchange_seq(d_wqkv.reshape(nseq, r, 3 * hw))
    grad_qkv = jnp.transpose(grad_qkv.reshape(nseq, r, 3, hw), (1, 2, 0, 3)).reshape(-1)

    zero = jnp.zeros((width,), F32)
    d_vec = jnp.concatenate(
        [
            lax.dynamic_update_slice_in_dim(zero, d_q_bias, s * hw, 0),
            lax.dynamic_update_slice_in_dim(zero, d_v_bias, s * hw, 0),
            d_o_bias,
            d_gain_one,
            d_shift_one,
            d_down_bias,
            d_gain_two,
            d_shift_two,
            lax.dynamic_update_slice_in_dim(jnp.zeros((hidden,), F32), d_up_bias, s * hid, 0),
        ]
    )
    if lax.axis_size("z") > 8:
        grad_vectors = lax.psum_scatter(d_vec, ALL, scatter_dimension=0, tiled=True)
    else:
        vec = d_vec.reshape(nall, -1)
        for axis in ("core", "x", "y", "z"):
            n = lax.axis_size(axis)
            blocks = jnp.moveaxis(vec.reshape(-1, n, vec.shape[-1]), 1, 0)
            own, got = scatter_pieces(blocks, axis)
            vec = sum(got, own)
        grad_vectors = vec.reshape(-1)
    return (layer_output, input_grad, grad_qkv, grad_out, grad_up, grad_down, grad_vectors)


def solution(mesh):
    nf, ns = mesh.shape["fsdp"], mesh.shape["seq"]
    fine = Mesh(mesh.devices.reshape(nf // 2, 2, ns // 2, 2), ALL)
    acts = P(FSDP, SEQ, None)
    flat = P(ALL)
    return jax.shard_map(
        on_device,
        mesh=fine,
        in_specs=(acts, P(FSDP), flat, flat, flat, flat, flat, acts),
        out_specs=(acts, acts, flat, flat, flat, flat, flat),
        check_vma=False,
    )
```

```python
import functools
import math

import jax
import jax.numpy as jnp
from jax import lax
from jax.experimental import pallas as pl
from jax.experimental.pallas import tpu as pltpu
from jax.sharding import PartitionSpec as P

H = 12
NEG = -1e30
EPS = 1e-06
ROOT_HALF = 0.7071067811865476
INV_ROOT_TAU = 0.3989422804014327

BF = jnp.bfloat16
F32 = jnp.float32
SEQ = "seq"
FSDP = "fsdp"
ALL = ("fsdp", "seq")


def dot(a, b, ca, cb):
    return lax.dot_general(a, b, (((ca,), (cb,)), ((), ())), preferred_element_type=F32)


def swap(value, axis, mask):
    n = lax.axis_size(axis)
    return lax.ppermute(value, axis, [(i, i ^ mask) for i in range(n)])


def bits(n):
    return [1 << k for k in reversed(range(n.bit_length() - 1))]


def gather(value, axis):
    order = [0]
    out = value[None]
    for mask in bits(lax.axis_size(axis)):
        out = jnp.concatenate([out, swap(out, axis, mask)])
        order = order + [e ^ mask for e in order]
    return out, order


def order_of(n):
    order = [0]
    for mask in bits(n):
        order = order + [e ^ mask for e in order]
    return order


def reduce(blocks, axis):
    for mask in reversed(bits(lax.axis_size(axis))):
        half = blocks.shape[0] // 2
        blocks = blocks[:half] + swap(blocks[half:].astype(BF), axis, mask).astype(F32)
    return blocks[0]


def reorder_kernel(order, me_ref, x_ref, o_ref):
    for e, rel in enumerate(order):
        o_ref[e] = x_ref[me_ref[0] ^ rel]


def place_kernel(order, me_ref, x_ref, o_ref):
    for e, rel in enumerate(order):
        o_ref[me_ref[0] ^ rel] = x_ref[e]


def moved(body, blocks, me):
    order = order_of(blocks.shape[0])
    vmem = pl.BlockSpec(memory_space=pltpu.VMEM)
    return pl.pallas_call(
        functools.partial(body, order),
        out_shape=jax.ShapeDtypeStruct(blocks.shape, blocks.dtype),
        in_specs=[pl.BlockSpec(memory_space=pltpu.SMEM), vmem],
        out_specs=vmem,
        name=body.__name__,
    )(me.reshape(1), blocks)


def exchange(blocks, axis):
    n = lax.axis_size(axis)
    return jnp.stack(
        [blocks[e] if rel == 0 else swap(blocks[e], axis, rel) for e, rel in enumerate(order_of(n))]
    )


def layer_norm(value):
    center = value - jnp.mean(value, axis=-1, keepdims=True)
    rstd = lax.rsqrt(jnp.mean(center * center, axis=-1, keepdims=True) + EPS)
    return center * rstd, rstd


def norm_back(grad, normed, rstd, gain):
    scaled = grad * gain
    return rstd * (
        scaled
        - jnp.mean(scaled, axis=-1, keepdims=True)
        - normed * jnp.mean(scaled * normed, axis=-1, keepdims=True)
    )


def on_device(layer_input, valid_lengths, w_qkv, w_out, w_up, w_down, vectors, cotangent):
    batch, rows, width = layer_input.shape
    assert batch == 1
    nseq = lax.axis_size(SEQ)
    nf = lax.axis_size(FSDP)
    nall = nseq * nf
    s = lax.axis_index(SEQ)
    f = lax.axis_index(FSDP)
    span = rows * nseq
    hidden = w_up.shape[0] * nall // width
    head = width // H
    mine = H // nseq
    hw = mine * head
    hid = hidden // nseq
    scale = 1.0 / math.sqrt(head)
    into = [(b, (b % nf) * nseq + b // nf) for b in range(nall)]
    back = [(d, b) for b, d in into]
    near = order_of(nseq)

    r = width // nall
    hr = hidden // nall
    tokens = layer_input.reshape(rows, width)
    x_full = gather(tokens, SEQ)[0].reshape(span, width)

    def columns(blocks):
        got = exchange(moved(reorder_kernel, blocks, s), SEQ)
        got = moved(place_kernel, got, s)
        got = got.reshape(nseq * r, -1)
        full = moved(place_kernel, gather(got, FSDP)[0], f)
        return full.reshape(width, -1)

    def rows_of(mine_rows):
        full = moved(place_kernel, gather(mine_rows, FSDP)[0], f)
        return full.reshape(-1, width)

    wqkv = columns(
        jnp.transpose(w_qkv.reshape(r, 3, nseq, hw), (2, 0, 1, 3)).reshape(nseq, r, 3 * hw)
    )
    wo = rows_of(lax.ppermute(w_out.reshape(r, width), ALL, into))
    w1 = columns(
        jnp.transpose(w_up.reshape(r, nf, nseq, hr), (2, 0, 1, 3)).reshape(nseq, r, hid)
    )
    w2 = rows_of(w_down.reshape(hr, width))

    vec = gather(vectors, SEQ)[0][:, None, :]
    vec = moved(place_kernel, vec, s).reshape(-1)
    vec = gather(vec, FSDP)[0][:, None, :]
    flat = moved(place_kernel, vec, f).reshape(-1).astype(F32)
    q_bias, v_bias, o_bias, gain_one, shift_one, down_bias, gain_two, shift_two = [
        flat[i * width : (i + 1) * width] for i in range(8)
    ]
    up_bias = flat[8 * width :].reshape(nf, nseq, hr)
    up_bias = lax.dynamic_index_in_dim(up_bias, s, 1, keepdims=False).reshape(hid)
    q_bias = lax.dynamic_slice_in_dim(q_bias, s * hw, hw)
    v_bias = lax.dynamic_slice_in_dim(v_bias, s * hw, hw)

    def gather_seq(value):
        return gather(value, SEQ)[0].reshape(span, width)

    def reduce_seq(part):
        return reduce(part.reshape(nseq, rows, width), SEQ)

    def reduce_fsdp(part):
        return reduce(moved(reorder_kernel, part.reshape(nf, -1, part.shape[-1]), f), FSDP)

    def exchange_seq(part):
        blocks = part.reshape(nseq, r, part.shape[-1])
        got = exchange(moved(reorder_kernel, blocks, s), SEQ)
        return moved(place_kernel, got, s)

    qkv = dot(x_full, wqkv, 1, 0) + jnp.concatenate([q_bias, jnp.zeros_like(q_bias), v_bias])
    query = qkv[:, :hw].astype(BF)
    keys = qkv[:, hw : 2 * hw].astype(BF)
    values = qkv[:, 2 * hw :].astype(BF)
    offsets = jnp.stack([(s ^ e) * rows for e in near])
    places = (offsets[:, None] + jnp.arange(rows)[None, :]).reshape(span)
    keep = places < valid_lengths[0]
    qh = query.reshape(span, mine, head)
    kh = keys.reshape(span, mine, head)
    vh = values.reshape(span, mine, head)
    scores = jnp.einsum("qhd,khd->hqk", qh, kh, preferred_element_type=F32) * scale
    scores = jnp.where(keep[None, None, :], scores, NEG)
    top = jnp.max(scores, axis=-1, keepdims=True)
    expo = jnp.exp(scores - top)
    total = jnp.sum(expo, axis=-1, keepdims=True)
    lse = top + jnp.log(total)
    probs = (expo / total).astype(BF)
    context = jnp.einsum("hqk,khd->qhd", probs, vh, preferred_element_type=F32)
    context = context.reshape(span, hw).astype(BF)

    first = tokens.astype(F32) + reduce_seq(dot(context, wo, 1, 0)) + o_bias
    normed_one, rstd_one = layer_norm(first)
    mid = normed_one * gain_one + shift_one
    mid_b = gather_seq(mid.astype(BF))
    upper = dot(mid_b, w1, 1, 0) + up_bias
    cdf = 0.5 * (1.0 + lax.erf(upper * ROOT_HALF))
    active = (upper * cdf).astype(BF)
    second = mid + reduce_seq(dot(active, w2, 1, 0)) + down_bias
    normed_two, rstd_two = layer_norm(second)
    layer_output = (normed_two * gain_two + shift_two).astype(BF).reshape(batch, rows, width)

    grad = cotangent.reshape(rows, width).astype(F32)
    d_gain_two = jnp.sum(grad * normed_two, axis=0)
    d_shift_two = jnp.sum(grad, axis=0)
    d_second = norm_back(grad, normed_two, rstd_two, gain_two)
    d_down_bias = jnp.sum(d_second, axis=0)
    d_second_b = gather_seq(d_second.astype(BF))
    slope = cdf + upper * jnp.exp(-0.5 * upper * upper) * INV_ROOT_TAU
    d_upper = dot(d_second_b, w2, 1, 1) * slope
    d_up_bias = jnp.sum(d_upper, axis=0)
    d_upper_b = d_upper.astype(BF)
    d_mid = d_second + reduce_seq(dot(d_upper_b, w1, 1, 1))
    d_w2 = reduce_fsdp(dot(active, d_second_b, 0, 0))
    d_w1 = reduce_fsdp(dot(mid_b, d_upper_b, 0, 0))
    grad_down = d_w2.reshape(-1)
    grad_up = exchange_seq(d_w1).reshape(nseq, r, nf, hr)
    grad_up = jnp.transpose(grad_up, (1, 2, 0, 3)).reshape(-1)

    d_gain_one = jnp.sum(d_mid * normed_one, axis=0)
    d_shift_one = jnp.sum(d_mid, axis=0)
    d_first = norm_back(d_mid, normed_one, rstd_one, gain_one)
    d_o_bias = jnp.sum(d_first, axis=0)
    d_first_b = gather_seq(d_first.astype(BF))
    d_context = dot(d_first_b, wo, 1, 1).astype(BF)
    d_wo = reduce_fsdp(dot(context, d_first_b, 0, 0))
    grad_out = lax.ppermute(d_wo, ALL, back).reshape(-1)

    dch = d_context.reshape(span, mine, head)
    cth = context.reshape(span, mine, head)
    prob = jnp.exp(scores - lse)
    prob_b = prob.astype(BF)
    d_vh = jnp.einsum("hqk,qhd->khd", prob_b, dch, preferred_element_type=F32)
    d_prob = jnp.einsum("qhd,khd->hqk", dch, vh, preferred_element_type=F32)
    delta = jnp.sum(dch.astype(F32) * cth.astype(F32), axis=-1)
    delta = jnp.transpose(delta, (1, 0))[:, :, None]
    d_scores = (prob * (d_prob - delta) * scale).astype(BF)
    d_qh = jnp.einsum("hqk,khd->qhd", d_scores, kh, preferred_element_type=F32)
    d_kh = jnp.einsum("hqk,qhd->khd", d_scores, qh, preferred_element_type=F32)
    d_q = d_qh.reshape(span, hw)
    d_k = d_kh.reshape(span, hw)
    d_v = d_vh.reshape(span, hw)
    d_q_bias = jnp.sum(d_q, axis=0)
    d_v_bias = jnp.sum(d_v, axis=0)
    d_qkv = jnp.concatenate([d_q, d_k, d_v], axis=1).astype(BF)
    input_grad = d_first + reduce_seq(dot(d_qkv, wqkv, 1, 1))
    input_grad = input_grad.reshape(batch, rows, width)
    d_wqkv = reduce_fsdp(dot(x_full, d_qkv, 0, 0))
    grad_qkv = exchange_seq(d_wqkv)
    grad_qkv = jnp.transpose(grad_qkv.reshape(nseq, r, 3, hw), (1, 2, 0, 3)).reshape(-1)

    zero = jnp.zeros((width,), F32)
    d_vec = jnp.concatenate(
        [
            lax.dynamic_update_slice_in_dim(zero, d_q_bias, s * hw, 0),
            lax.dynamic_update_slice_in_dim(zero, d_v_bias, s * hw, 0),
            d_o_bias,
            d_gain_one,
            d_shift_one,
            d_down_bias,
            d_gain_two,
            d_shift_two,
            jnp.where(
                jnp.arange(nseq)[None, :, None] == s, d_up_bias.reshape(nf, 1, hr), 0.0
            ).reshape(-1),
        ]
    )
    vec = moved(reorder_kernel, d_vec.reshape(nf, 1, -1), f)[:, 0]
    for mask in reversed(bits(nf)):
        half = vec.shape[0] // 2
        vec = vec[:half] + swap(vec[half:], FSDP, mask)
    vec = moved(reorder_kernel, vec.reshape(nseq, 1, -1), s)[:, 0]
    for mask in reversed(bits(nseq)):
        half = vec.shape[0] // 2
        vec = vec[:half] + swap(vec[half:], SEQ, mask)
    grad_vectors = vec.reshape(-1)
    return (layer_output, input_grad, grad_qkv, grad_out, grad_up, grad_down, grad_vectors)


def solution(mesh):
    acts = P(FSDP, SEQ, None)
    flat = P(ALL)
    return jax.shard_map(
        on_device,
        mesh=mesh,
        in_specs=(acts, P(FSDP), flat, flat, flat, flat, flat, acts),
        out_specs=(acts, acts, flat, flat, flat, flat, flat),
        check_vma=False,
    )
```

```python
import functools
import math

import jax
import jax.numpy as jnp
from jax import lax
from jax.experimental import pallas as pl
from jax.experimental.pallas import tpu as pltpu
from jax.sharding import PartitionSpec as P

H = 12
NEG = -1e30
EPS = 1e-06
ROOT_HALF = 0.7071067811865476
INV_ROOT_TAU = 0.3989422804014327

BF = jnp.bfloat16
F32 = jnp.float32
SEQ = "seq"
FSDP = "fsdp"
ALL = ("fsdp", "seq")
LANES = 128


def dot(a, b, ca, cb):
    return lax.dot_general(a, b, (((ca,), (cb,)), ((), ())), preferred_element_type=F32)


def up16(n):
    return -(-n // 16) * 16


def swap(value, axis, mask):
    n = lax.axis_size(axis)
    return lax.ppermute(value, axis, [(i, i ^ mask) for i in range(n)])


def bits(n):
    return [1 << k for k in reversed(range(n.bit_length() - 1))]


def order_of(n):
    order = [0]
    for mask in bits(n):
        order = order + [e ^ mask for e in order]
    return order


def gather(value, axis):
    n = lax.axis_size(axis)
    if n > 8:
        out = value[None]
        for mask in bits(n):
            out = jnp.concatenate([out, swap(out, axis, mask)])
        got = dict(zip(order_of(n), out))
        return [got[e] for e in range(n)]
    got = {0: value}
    for mask in bits(n):
        for e in list(got):
            got[e ^ mask] = swap(got[e], axis, mask)
    return [got[e] for e in range(n)]


def exchange(blocks, axis):
    return [b if e == 0 else swap(b, axis, e) for e, b in enumerate(blocks)]


def call(body, outs, info, args, scratch=()):
    vmem = pl.BlockSpec(memory_space=pltpu.VMEM)
    name = getattr(body, "func", body).__name__
    return pl.pallas_call(
        body,
        out_shape=[jax.ShapeDtypeStruct(s, d) for s, d in outs],
        in_specs=[pl.BlockSpec(memory_space=pltpu.SMEM)] + [vmem] * len(args),
        out_specs=[vmem] * len(outs),
        scratch_shapes=[pltpu.VMEM(s, d) for s, d in scratch],
        name=name,
    )(info, *args)


def pieces_of(start, count, width):
    done = 0
    while done < count:
        row, col = divmod(start + done, width)
        take = min(width - col, count - done)
        yield row, col, done, take
        done += take


def store_rows(out_ref, value):
    r, w = value.shape
    tiles = w // LANES
    for t in range(tiles):
        out_ref[pl.ds(t, r, stride=tiles), :] = value[:, t * LANES : (t + 1) * LANES]


def pack_inputs(dims, info, wq, wu, vec, q0, q1, q2, q3, u0, u1, u2, u3, sq, su):
    r, hw, hr, nf, ns, width, nv = dims
    s = info[0]
    for j in range(ns):
        for p in range(3):
            sq[j, 0:r, p * hw : (p + 1) * hw] = wq[:, p * width + j * hw : p * width + (j + 1) * hw]
        sq[j, r : r + 1, 0:nv] = vec[...]
        for b in range(nf):
            c = (b * ns + j) * hr
            su[j, :, b * hr : (b + 1) * hr] = wu[:, c : c + hr]
    for e, (q, u) in enumerate(((q0, u0), (q1, u1), (q2, u2), (q3, u3))):
        q[...] = sq[s ^ e]
        u[...] = su[s ^ e]


def pack_first(dims, info, q0, q1, q2, q3, wo, out, sq):
    r, hw, hr, nf, ns, width, nv = dims
    s = info[0]
    for e, q in enumerate((q0, q1, q2, q3)):
        sq[s ^ e] = q[...]
    for j in range(ns):
        out[j * r : (j + 1) * r, 0 : 3 * hw] = sq[j, 0:r, :]
        out[j * r : (j + 1) * r, 3 * hw : 4 * hw] = wo[:, j * hw : (j + 1) * hw]
        out[ns * r + j : ns * r + j + 1, 0:nv] = sq[j, r : r + 1, 0:nv]


def pack_second(dims, info, u0, u1, u2, u3, wd, out, su):
    r, hw, hr, nf, ns, width, nv = dims
    s = info[0]
    for e, u in enumerate((u0, u1, u2, u3)):
        su[s ^ e] = u[...]
    for j in range(ns):
        out[j * r : (j + 1) * r, :] = su[j]
    out[ns * r : ns * r + hr, :] = wd[...]


def key_mask(info, near, rows, span):
    col = lax.broadcasted_iota(jnp.int32, (1, span), 1)
    blk = col // rows
    rel = jnp.zeros_like(col)
    for i, e in enumerate(near):
        rel = jnp.where(blk == i, e, rel)
    place = (rel ^ info[0]) * rows + (col - blk * rows)
    return place < info[2]


def attention(dims, near, info, *refs):
    r, hw, hr, nf, ns, width, nv = dims
    xs, ps = refs[:ns], refs[ns : ns + nf]
    x_ref, wq_ref, wo_ref, vec_ref, qkv_ref, ctx_ref, lse_ref, send, keep = refs[ns + nf : ns + nf + 9]
    s3, so, sv, sb, sbias = refs[ns + nf + 9 :]
    s, f = info[0], info[1]
    rows = xs[0].shape[0]
    span = rows * ns
    head = width // H
    heads = hw // head
    block = ns * r
    for i in range(ns):
        x_ref[i * rows : (i + 1) * rows, :] = xs[i][...]
    for e in range(nf):
        s3[f ^ e] = ps[e][0:block, 0 : 3 * hw]
        so[f ^ e] = ps[e][0:block, 3 * hw : 4 * hw]
        sv[f ^ e] = ps[e][block : block + ns, 0:nv].astype(F32)
    for b in range(nf):
        wq_ref[b * block : (b + 1) * block, :] = s3[b]
        for c in range(ns):
            wo_ref[b * r : (b + 1) * r, c * hw : (c + 1) * hw] = so[b, c * r : (c + 1) * r, :]
            start = (b * ns + c) * nv
            for row, col, off, take in pieces_of(start, nv, width):
                vec_ref[row : row + 1, col : col + take] = sv[b, c : c + 1, off : off + take]
    for j in range(ns):
        for b in range(nf):
            row, col = divmod((b * ns + j) * hr, width)
            sb[j, :, b * hr : (b + 1) * hr] = vec_ref[8 + row : 9 + row, col : col + hr]
        sbias[j, :, 0:hw] = vec_ref[0:1, j * hw : (j + 1) * hw]
        sbias[j, :, hw : 2 * hw] = jnp.zeros((1, hw), F32)
        sbias[j, :, 2 * hw : 3 * hw] = vec_ref[1:2, j * hw : (j + 1) * hw]
    vec_ref[8:9, :] = sb[s]
    qkv = dot(x_ref[...], wq_ref[...], 1, 0) + sbias[s]
    qkv_ref[...] = qkv.astype(BF)
    mask = key_mask(info, near, rows, span)
    for h in range(heads):
        q = qkv_ref[:, h * head : (h + 1) * head]
        k = qkv_ref[:, hw + h * head : hw + (h + 1) * head]
        v = qkv_ref[:, 2 * hw + h * head : 2 * hw + (h + 1) * head]
        scores = jnp.where(mask, dot(q, k, 1, 1) * (1.0 / math.sqrt(head)), NEG)
        top = jnp.max(scores, axis=-1, keepdims=True)
        expo = jnp.exp(scores - top)
        total = jnp.sum(expo, axis=-1, keepdims=True)
        lse_ref[h] = top + jnp.log(total)
        probs = (expo * (1.0 / total)).astype(BF)
        ctx_ref[:, h * head : (h + 1) * head] = dot(probs, v, 1, 0).astype(BF)
    part = dot(ctx_ref[...], wo_ref[...], 1, 0)
    keep[...] = part[: span // 2]
    send[...] = part[span // 2 :].astype(BF)


def fold(info, keep, got, send):
    half = keep.shape[0] // 2
    send[...] = (keep[half:, :] + got[half:, :].astype(F32)).astype(BF)


def summed(keep, got, last):
    half = keep.shape[0] // 2
    return keep[0:half, :] + got[0:half, :].astype(F32) + last[...].astype(F32)


def mean(value):
    return jnp.mean(value, axis=-1, keepdims=True)


def norm_one(info, x, keep, got, last, vec, mid_ref, mid_b, normed_ref, rstd_ref):
    first = x[...].astype(F32) + summed(keep, got, last) + vec[2:3, :]
    center = first - mean(first)
    rstd = lax.rsqrt(mean(center * center) + EPS)
    normed = center * rstd
    mid = normed * vec[3:4, :] + vec[4:5, :]
    normed_ref[...] = normed
    rstd_ref[...] = rstd
    mid_ref[...] = mid
    mid_b[...] = mid.astype(BF)


def feed_forward(dims, info, *refs):
    r, hw, hr, nf, ns, width, nv = dims
    ms, ps = refs[:ns], refs[ns : ns + nf]
    vec, m_ref, w1_ref, w2_ref, u_ref, g_ref, send, keep, s3 = refs[ns + nf :]
    f = info[1]
    rows = ms[0].shape[0]
    block = ns * r
    for i in range(ns):
        m_ref[i * rows : (i + 1) * rows, :] = ms[i][...]
    for e in range(nf):
        s3[f ^ e] = ps[e][...]
    for b in range(nf):
        w1_ref[b * block : (b + 1) * block, :] = s3[b, 0:block, :]
        w2_ref[b * hr : (b + 1) * hr, :] = s3[b, block : block + hr, :]
    upper = dot(m_ref[...], w1_ref[...], 1, 0) + vec[8:9, :]
    u_ref[...] = upper
    g_ref[...] = (0.5 * upper * (1.0 + lax.erf(upper * ROOT_HALF))).astype(BF)
    part = dot(g_ref[...], w2_ref[...], 1, 0)
    half = part.shape[0] // 2
    keep[...] = part[:half]
    send[...] = part[half:].astype(BF)


def slope_of(info, u, out):
    value = u[...]
    out[...] = (
        0.5 * (1.0 + lax.erf(value * ROOT_HALF))
        + value * jnp.exp(-0.5 * value * value) * INV_ROOT_TAU
    )


def column_sum(value):
    return jnp.sum(value, axis=0, keepdims=True)


def norm_back(grad, normed, rstd, gain):
    scaled = grad * gain
    return rstd * (scaled - mean(scaled) - normed * mean(scaled * normed))


def norm_two(info, mid, keep, got, last, vec, cot, out, d_ref, d_b, sums):
    second = mid[...] + summed(keep, got, last) + vec[5:6, :]
    center = second - mean(second)
    rstd = lax.rsqrt(mean(center * center) + EPS)
    normed = center * rstd
    gain = vec[6:7, :]
    out[...] = (normed * gain + vec[7:8, :]).astype(BF)
    grad = cot[...].astype(F32)
    d_second = norm_back(grad, normed, rstd, gain)
    d_ref[...] = d_second
    d_b[...] = d_second.astype(BF)
    sums[0:1, :] = column_sum(d_second)
    sums[1:2, :] = column_sum(grad * normed)
    sums[2:3, :] = column_sum(grad)


def feed_back(info, *refs):
    ds = refs[:-8]
    slope, w1, w2, d_ref, du_ref, db, send, keep = refs[-8:]
    rows = ds[0].shape[0]
    for i, d in enumerate(ds):
        d_ref[i * rows : (i + 1) * rows, :] = d[...]
    d_upper = dot(d_ref[...], w2[...], 1, 1) * slope[...]
    db[...] = column_sum(d_upper)
    du_ref[...] = d_upper.astype(BF)
    part = dot(du_ref[...], w1[...], 1, 1)
    half = part.shape[0] // 2
    keep[...] = part[:half]
    send[...] = part[half:].astype(BF)


def relative(order, f, blocks, send, keep):
    half = len(order) // 2
    for i in range(half):
        keep[i] = blocks[f ^ order[i]]
        send[i] = blocks[f ^ order[half + i]].astype(BF)


def feed_grads(dims, order, info, mid, du, act, d, send, keep, blocks):
    r, hw, hr, nf, ns, width, nv = dims
    block = ns * r
    d_w1 = dot(mid[...], du[...], 0, 0)
    for b in range(nf):
        blocks[b, 0:block, :] = d_w1[b * block : (b + 1) * block]
    d_w2 = dot(act[...], d[...], 0, 0)
    for b in range(nf):
        blocks[b, block : block + hr, :] = d_w2[b * hr : (b + 1) * hr]
    relative(order, info[1], blocks, send, keep)


def norm_one_back(info, d2, keep, got, last, normed_ref, rstd, vec, d_ref, d_b, sums):
    d_mid = d2[...] + summed(keep, got, last)
    normed = normed_ref[...]
    d_first = norm_back(d_mid, normed, rstd[...], vec[3:4, :])
    d_ref[...] = d_first
    d_b[...] = d_first.astype(BF)
    sums[0:1, :] = column_sum(d_first)
    sums[1:2, :] = column_sum(d_mid * normed)
    sums[2:3, :] = column_sum(d_mid)


def attention_back(dims, near, info, *refs):
    r, hw, hr, nf, ns, width, nv = dims
    das = refs[:ns]
    wo, wq, ctx, qkv, lse, da_ref, dqkv_ref, db, send, keep, dc_ref = refs[ns:]
    rows = das[0].shape[0]
    span = rows * ns
    head = width // H
    scale = 1.0 / math.sqrt(head)
    for i in range(ns):
        da_ref[i * rows : (i + 1) * rows, :] = das[i][...]
    dc_ref[...] = dot(da_ref[...], wo[...], 1, 1).astype(BF)
    mask = key_mask(info, near, rows, span)
    for h in range(hw // head):
        at = slice(h * head, (h + 1) * head)
        q = qkv[:, h * head : (h + 1) * head]
        k = qkv[:, hw + h * head : hw + (h + 1) * head]
        v = qkv[:, 2 * hw + h * head : 2 * hw + (h + 1) * head]
        dc = dc_ref[:, at]
        scores = jnp.where(mask, dot(q, k, 1, 1) * scale, NEG)
        prob = jnp.exp(scores - lse[h])
        d_v = dot(prob.astype(BF), dc, 0, 0)
        delta = jnp.sum(dc.astype(F32) * ctx[:, at].astype(F32), axis=-1, keepdims=True)
        d_s = (prob * (dot(dc, v, 1, 1) - delta) * scale).astype(BF)
        d_q = dot(d_s, k, 1, 0)
        d_k = dot(d_s, q, 0, 0)
        dqkv_ref[:, h * head : (h + 1) * head] = d_q.astype(BF)
        dqkv_ref[:, hw + h * head : hw + (h + 1) * head] = d_k.astype(BF)
        dqkv_ref[:, 2 * hw + h * head : 2 * hw + (h + 1) * head] = d_v.astype(BF)
        db[0:1, at] = column_sum(d_q)
        db[1:2, at] = column_sum(d_v)
    part = dot(dqkv_ref[...], wq[...], 1, 1)
    keep[...] = part[: span // 2]
    send[...] = part[span // 2 :].astype(BF)


def attention_grads(
    dims, order, info, x, dqkv, ctx, da, db, sums_one, sums_two, db_up, send, keep, blocks, flat
):
    r, hw, hr, nf, ns, width, nv = dims
    s = info[0]
    block = ns * r
    d_wq = dot(x[...], dqkv[...], 0, 0)
    for b in range(nf):
        blocks[b, 0:block, 0 : 3 * hw] = d_wq[b * block : (b + 1) * block]
    d_wo = dot(ctx[...], da[...], 0, 0)
    for b in range(nf):
        for c in range(ns):
            blocks[b, c * r : (c + 1) * r, 3 * hw : 4 * hw] = d_wo[
                b * r : (b + 1) * r, c * hw : (c + 1) * hw
            ]
    for j in range(ns):
        for i in range(2):
            flat[i : i + 1, j * hw : (j + 1) * hw] = jnp.where(s == j, db[i : i + 1, :], 0.0)
        for b in range(nf):
            row, col = divmod((b * ns + j) * hr, width)
            flat[8 + row : 9 + row, col : col + hr] = jnp.where(
                s == j, db_up[0:1, b * hr : (b + 1) * hr], 0.0
            )
    flat[2:5, :] = sums_one[0:3, :]
    flat[5:8, :] = sums_two[0:3, :]
    for b in range(nf):
        for c in range(ns):
            for row, col, off, take in pieces_of((b * ns + c) * nv, nv, width):
                blocks[b, block + c : block + c + 1, off : off + take] = flat[
                    row : row + 1, col : col + take
                ]
    relative(order, info[1], blocks, send, keep)


def fold_blocks(info, keep, got, send, left):
    half = keep.shape[0] // 2
    left[...] = keep[0:half] + got[0:half].astype(F32)
    send[...] = (keep[half:] + got[half:].astype(F32)).astype(BF)


def reduce_blocks(info, send, keep):
    mask = 1
    while True:
        got = swap(send, FSDP, mask)
        n, rows, width = keep.shape
        if n == 1:
            return keep, got
        shape = (n // 2, rows, width)
        send, keep = call(fold_blocks, [(shape, BF), (shape, F32)], info, [keep, got])
        mask *= 2


def split_up(dims, info, keep, got, down, v0, v1, v2, v3, sv):
    r, hw, hr, nf, ns, width, nv = dims
    total = keep[0] + got[0].astype(F32)
    for j in range(ns):
        sv[j] = total[j * r : (j + 1) * r]
    for e, v in enumerate((v0, v1, v2, v3)):
        v[...] = sv[info[0] ^ e]
    store_rows(down, total[ns * r : ns * r + hr])


def join_up(dims, info, v0, v1, v2, v3, out, sv, sm):
    r, hw, hr, nf, ns, width, nv = dims
    for e, v in enumerate((v0, v1, v2, v3)):
        sv[info[0] ^ e] = v[...]
    for j in range(ns):
        for b in range(nf):
            c = (b * ns + j) * hr
            sm[:, c : c + hr] = sv[j, :, b * hr : (b + 1) * hr]
    store_rows(out, sm[...])


def split_qkv(dims, info, keep, got, wo, q0, q1, q2, q3, sq):
    r, hw, hr, nf, ns, width, nv = dims
    total = keep[0] + got[0].astype(F32)
    for j in range(ns):
        wo[:, j * hw : (j + 1) * hw] = total[j * r : (j + 1) * r, 3 * hw : 4 * hw]
        sq[j, 0:r, :] = total[j * r : (j + 1) * r, 0 : 3 * hw]
        sq[j, r : r + 1, 0:nv] = total[ns * r + j : ns * r + j + 1, 0:nv]
    for e, q in enumerate((q0, q1, q2, q3)):
        q[...] = sq[info[0] ^ e]


def join_qkv(dims, info, q0, q1, q2, q3, wo, out, out_wo, out_vec, sq, sm):
    r, hw, hr, nf, ns, width, nv = dims
    for e, q in enumerate((q0, q1, q2, q3)):
        sq[info[0] ^ e] = q[...]
    vec = jnp.zeros((1, nv), F32)
    for j in range(ns):
        for p in range(3):
            sm[:, p * width + j * hw : p * width + (j + 1) * hw] = sq[j, 0:r, p * hw : (p + 1) * hw]
        vec = vec + sq[j, r : r + 1, 0:nv]
    store_rows(out, sm[...])
    store_rows(out_wo, wo[...])
    out_vec[...] = vec


def last_sum(info, d_first, keep, got, last, out):
    out[...] = d_first[...] + summed(keep, got, last)


def on_device(layer_input, valid_lengths, w_qkv, w_out, w_up, w_down, vectors, cotangent):
    batch, rows, width = layer_input.shape
    assert batch == 1
    ns = lax.axis_size(SEQ)
    nf = lax.axis_size(FSDP)
    assert ns == 4
    nall = ns * nf
    s = lax.axis_index(SEQ)
    f = lax.axis_index(FSDP)
    span = rows * ns
    half = span // 2
    hidden = w_up.shape[0] * nall // width
    head = width // H
    hw = H // ns * head
    hid = hidden // ns
    r = width // nall
    hr = hidden // nall
    nv = vectors.shape[0]
    near = order_of(ns)
    order = order_of(nf)
    dims = (r, hw, hr, nf, ns, width, nv)
    into = [(b, (b % nf) * ns + b // nf) for b in range(nall)]
    back = [(d, b) for b, d in into]
    info = jnp.stack([s, f, valid_lengths[0]]).astype(jnp.int32)
    rq = up16(r + 1)
    g1 = up16(ns * r + ns)
    g2 = ns * r + hr

    def with_dims(body, *more):
        return functools.partial(named(body), dims, *more)

    def named(body):
        return body

    tokens = layer_input.reshape(rows, width)
    cot = cotangent.reshape(rows, width)

    packed = call(
        with_dims(pack_inputs),
        [((rq, 3 * hw), BF)] * ns + [((r, hid), BF)] * ns,
        info,
        [w_qkv.reshape(r, 3 * width), w_up.reshape(r, hidden), vectors.reshape(1, nv)],
        [((ns, rq, 3 * hw), BF), ((ns, r, hid), BF)],
    )
    wo_rows = lax.ppermute(w_out.reshape(r, width), ALL, into)
    qs = exchange(packed[:ns], SEQ)
    us = exchange(packed[ns:], SEQ)
    (first_pack,) = call(
        with_dims(pack_first), [((g1, width), BF)], info, qs + [wo_rows], [((ns, rq, 3 * hw), BF)]
    )
    first_pieces = gather(first_pack, FSDP)
    (second_pack,) = call(
        with_dims(pack_second),
        [((g2, width), BF)],
        info,
        us + [w_down.reshape(hr, width)],
        [((ns, r, hid), BF)],
    )
    second_pieces = gather(second_pack, FSDP)

    def ordered(value):
        got = gather(value, SEQ)
        return [got[e] for e in near]

    xs = ordered(tokens)

    partial = [((half, width), BF), ((half, width), F32)]
    x_full, wqkv, wo, vec, qkv, ctx, lse, send, keep = call(
        with_dims(attention, near),
        [
            ((span, width), BF),
            ((width, 3 * hw), BF),
            ((hw, width), BF),
            ((16, width), F32),
            ((span, 3 * hw), BF),
            ((span, hw), BF),
            ((hw // head, span, 1), F32),
        ]
        + partial,
        info,
        xs + first_pieces,
        [
            ((nf, ns * r, 3 * hw), BF),
            ((nf, ns * r, hw), BF),
            ((nf, ns, nv), F32),
            ((ns, 1, hid), F32),
            ((ns, 1, 3 * hw), F32),
        ],
    )

    def reduce_seq(send, keep):
        got = swap(send, SEQ, 1)
        (send,) = call(fold, [((rows, width), BF)], info, [keep, got])
        return [keep, got, swap(send, SEQ, 2)]

    act = ((rows, width), F32)
    act_b = ((rows, width), BF)
    full_b = ((span, width), BF)
    mid, mid_b, normed, rstd = call(
        norm_one,
        [act, act_b, act, ((rows, 1), F32)],
        info,
        [tokens] + reduce_seq(send, keep) + [vec],
    )
    mid_full, w1, w2, upper, active, send, keep = call(
        with_dims(feed_forward),
        [full_b, ((width, hid), BF), ((hid, width), BF), ((span, hid), F32), ((span, hid), BF)]
        + partial,
        info,
        ordered(mid_b) + second_pieces + [vec],
        [((nf, g2, width), BF)],
    )
    (slope,) = call(slope_of, [((span, hid), F32)], info, [upper])
    layer_output, d_second, d_second_b, sums_two = call(
        norm_two,
        [act_b, act, act_b, ((8, width), F32)],
        info,
        [mid] + reduce_seq(send, keep) + [vec, cot],
    )
    d_full, d_upper, db_up, send, keep = call(
        feed_back,
        [full_b, ((span, hid), BF), ((1, hid), F32)] + partial,
        info,
        ordered(d_second_b) + [slope, w1, w2],
    )
    shape = (nf // 2, g2, width)
    up_send, up_keep = call(
        with_dims(feed_grads, order),
        [(shape, BF), (shape, F32)],
        info,
        [mid_full, d_upper, active, d_full],
        [((nf, g2, width), F32)],
    )
    d_first, d_first_b, sums_one = call(
        norm_one_back,
        [act, act_b, ((8, width), F32)],
        info,
        [d_second] + reduce_seq(send, keep) + [normed, rstd, vec],
    )
    da_full, d_qkv, db, send, keep = call(
        with_dims(attention_back, near),
        [full_b, ((span, 3 * hw), BF), ((8, hw), F32)] + partial,
        info,
        ordered(d_first_b) + [wo, wqkv, ctx, qkv, lse],
        [((span, hw), BF)],
    )
    shape = (nf // 2, g1, width)
    q_send, q_keep = call(
        with_dims(attention_grads, order),
        [(shape, BF), (shape, F32)],
        info,
        [x_full, d_qkv, ctx, da_full, db, sums_one, sums_two, db_up],
        [((nf, g1, width), F32), ((16, width), F32)],
    )
    (input_grad,) = call(last_sum, [act], info, [d_first] + reduce_seq(send, keep))

    row_f32 = ((r, hid), F32)
    down, *ups = call(
        with_dims(split_up),
        [((hr * width // LANES, LANES), F32)] + [row_f32] * ns,
        info,
        list(reduce_blocks(info, up_send, up_keep)),
        [((ns, r, hid), F32)],
    )
    (up,) = call(
        with_dims(join_up),
        [((r * hidden // LANES, LANES), F32)],
        info,
        exchange(ups, SEQ),
        [((ns, r, hid), F32), ((r, hidden), F32)],
    )
    d_wo, *qs = call(
        with_dims(split_qkv),
        [((r, width), F32)] + [((rq, 3 * hw), F32)] * ns,
        info,
        list(reduce_blocks(info, q_send, q_keep)),
        [((ns, rq, 3 * hw), F32)],
    )
    g_qkv, g_wo, g_vec = call(
        with_dims(join_qkv),
        [((r * 3 * width // LANES, LANES), F32), ((r * width // LANES, LANES), F32), ((1, nv), F32)],
        info,
        exchange(qs, SEQ) + [lax.ppermute(d_wo, ALL, back)],
        [((ns, rq, 3 * hw), F32), ((r, 3 * width), F32)],
    )
    return (
        layer_output.reshape(batch, rows, width),
        input_grad.reshape(batch, rows, width),
        g_qkv.reshape(-1),
        g_wo.reshape(-1),
        up.reshape(-1),
        down.reshape(-1),
        g_vec.reshape(-1),
    )


def solution(mesh):
    acts = P(FSDP, SEQ, None)
    flat = P(ALL)
    return jax.shard_map(
        on_device,
        mesh=mesh,
        in_specs=(acts, P(FSDP), flat, flat, flat, flat, flat, acts),
        out_specs=(acts, acts, flat, flat, flat, flat, flat),
        check_vma=False,
    )
```
